32 devices in a mesh: section: 2 (over core), seq: 2 (over x), shard: 8 (over z, y).
Axes of the slice: x: 2, y: 2, z: 4, core: 2. Of those that a mesh axis runs over, the one named last changes fastest.
Arguments:
- feed: bfloat16 [2, 3, 8, 512, 768], P('section', None, 'shard', 'seq'), may hold values from -6 to 6
- segment_ids: int32 [3, 8, 512], P(None, 'shard', 'seq'), may hold values from 0 to 3, never falling along the last dimension, each value on 1 to 256 neighbouring positions
- w_qkv: bfloat16 [2, 768, 2304], P('section', ('seq', 'shard')), may hold values from -0.21875 to 0.21875
- w_out: bfloat16 [2, 768, 768], P('section', ('seq', 'shard')), may hold values from -1.75 to 1.75
- w_up: bfloat16 [2, 768, 3072], P('section', ('seq', 'shard')), may hold values from -0.21875 to 0.21875
- w_down: bfloat16 [2, 3072, 768], P('section', ('seq', 'shard')), may hold values from -0.109375 to 0.109375
- biases: bfloat16 [2, 6, 768], P('section', None, ('seq', 'shard')), may hold values from -3 to 3
- up_bias: bfloat16 [2, 3072], P('section', ('seq', 'shard')), may hold values from -3 to 3
- gains: bfloat16 [2, 2, 768], P('section', None, ('seq', 'shard')), may hold values from 0.5 to 1.5
Outputs:
- section_out: bfloat16 [2, 3, 8, 512, 768], P('section', None, 'shard', 'seq')
- grad_w_qkv: float32 [2, 768, 2304], P('section', ('seq', 'shard'))
- grad_w_out: float32 [2, 768, 768], P('section', ('seq', 'shard'))
- grad_w_up: float32 [2, 768, 3072], P('section', ('seq', 'shard'))
- grad_w_down: float32 [2, 3072, 768], P('section', ('seq', 'shard'))
- grad_biases: float32 [2, 6, 768], P('section', None, ('seq', 'shard'))
- grad_up_bias: float32 [2, 3072], P('section', ('seq', 'shard'))
- grad_gains: float32 [2, 2, 768], P('section', None, ('seq', 'shard'))
The draws below stay inside these ranges and needn't reach their ends.
Inputs may be any that keep to these rules, and one draw needn't show every extreme that they name: `segment_ids`: along each sequence the clip ids never fall; every id from 0 to 3 occurs, each clip holds 1 to 256 frames, and one clip of each sequence holds exactly 256.
All inputs are finite; a program needn't handle non-finite values.
Results may differ from the reference program's by a relative error of at most 0.007.
Values may be sent and summed in bfloat16 or wider, within the bound.
A program may use at most 320 MiB of HBM per device.

```python
import math
import jax
import jax.numpy as jnp
import numpy as np
from jax import lax

D = 768
HEADS = 12
HEAD_DIM = 64
FF = 3072
LEN = 512
CLIPS = 4
MICRO = 3
BATCH = 8
MOST = 256
N_SECTION = 2


def level_of(key, dims, pieces, low, largest):
    factor_of, own = 1.0, jax.random.fold_in(key, 6)
    for axis_at, blocks in pieces:
        draws = jnp.exp(jax.random.uniform(jax.random.fold_in(own, axis_at), (blocks,), jnp.float32, low / len(pieces), largest / len(pieces)))
        factor_of = factor_of * jnp.repeat(draws, dims[axis_at] // blocks).reshape([-1 if axis == axis_at else 1 for axis in range(len(dims))])
    return factor_of


def length_profile(count, total, limit, skew):
    portions = [(1 << 20) // math.isqrt(grade ** skew) + 1 for grade in range(2, count + 1)]
    surplus, counts = total - limit - (count - 1), [1] * (count - 1)
    while surplus > 0:
        free = [i for i in range(count - 1) if counts[i] < limit]
        pool, budget = sum([portions[i] for i in free]), surplus
        for i in free:
            addition = min(limit - counts[i], max(1, budget * portions[i] // pool), surplus)
            counts[i] = counts[i] + addition
            surplus = surplus - addition
    return np.array([limit] + counts)


def uneven(key, count, total, limit, slope):
    if count == 2:
        one = jax.random.randint(key, (), max(1, total - limit), min(limit, total - 1) + 1)
        return jnp.stack([one, total - one])
    lengths = jnp.asarray(length_profile(count, total, limit, slope), jnp.int32)
    pairs = (count - 1) // 2
    source_of, taker = lengths[1:1 + 2 * pairs:2], lengths[2:2 + 2 * pairs:2]
    slack = jnp.minimum(source_of - 1, limit - taker)
    passed = jax.random.randint(jax.random.fold_in(key, 1), (pairs,), 0, 1 << 20) % (slack + 1)
    lengths = lengths.at[1:1 + 2 * pairs:2].set(source_of - passed).at[2:2 + 2 * pairs:2].set(taker + passed)
    return lengths[jax.random.permutation(jax.random.fold_in(key, 2), count)]


def noise(own_key, shape, width, reach, cuts=(), dtype=jnp.bfloat16):
    values = width * jax.random.normal(own_key, shape, jnp.float32)
    if cuts:
        values = values * level_of(own_key, shape, cuts, -0.22, 0.18)
    return jnp.clip(values, -reach, reach).astype(dtype)


def setup_inputs(seed: int = 0) -> dict:
    seeds = jax.random.split(jax.random.key(seed), 10)
    return {
        "feed": noise(seeds[0], (N_SECTION, MICRO, BATCH, LEN, D), 1.0, 6.0, ((0, 2), (2, 8), (3, 2))),
        "segment_ids": jax.vmap(lambda own: jnp.searchsorted(jnp.cumsum(uneven(own, CLIPS, LEN, MOST, 2)), jnp.arange(LEN), side="right"))(jax.random.split(seeds[1], MICRO * BATCH)).reshape((MICRO, BATCH, LEN)).astype(jnp.int32),
        "w_qkv": noise(seeds[2], (N_SECTION, D, 3 * D), D ** -0.5, 0.21875, ((0, 2), (1, 16))),
        "w_out": noise(seeds[3], (N_SECTION, D, D), (D // 64) ** -0.5, 1.75, ((0, 2), (1, 16))),
        "w_up": noise(seeds[4], (N_SECTION, D, FF), D ** -0.5, 0.21875, ((0, 2), (1, 16))),
        "w_down": noise(seeds[5], (N_SECTION, FF, D), FF ** -0.5, 0.109375, ((0, 2), (1, 16))),
        "biases": noise(seeds[6], (N_SECTION, 6, D), 0.5, 3.0, ((0, 2), (2, 16))),
        "up_bias": noise(seeds[7], (N_SECTION, FF), 0.5, 3.0, ((0, 2), (1, 16))),
        "gains": jnp.clip(1.0 + 0.1 * jax.random.normal(seeds[8], (N_SECTION, 2, D), jnp.float32), 0.5, 1.5).astype(jnp.bfloat16),
    }


highest = lax.Precision.HIGHEST
epsilon = 1e-05
neg_big = -1000000000.0

@jax.custom_vjp
def low(v):
    return lax.optimization_barrier(v.astype(jnp.bfloat16)).astype(jnp.float32)

@jax.custom_vjp
def low_back(v):
    return v

def low_keep(v):
    return (low(v), None)

def low_pass(kept, grad):
    return (grad,)

def back_keep(v):
    return (v, None)

def back_low(kept, grad):
    return (low(grad),)
low.defvjp(low_keep, low_pass)
low_back.defvjp(back_keep, back_low)

def norm_apply(values, gain_row, shift_row):
    row_mean = lax.optimization_barrier(jnp.mean(values, axis=-1, keepdims=True))
    centred = values - row_mean
    variance = lax.optimization_barrier(jnp.mean(centred * centred, axis=-1, keepdims=True))
    return centred * lax.rsqrt(variance + epsilon) * gain_row + shift_row

def gelu_exact(values):
    return 0.5 * values * (1.0 + lax.erf(values * 2.0 ** (-0.5)))

def encoder_layer(inputs, clip_row, w_qkv, w_out, w_up, w_down, biases, up_bias, gains):
    feat_width = inputs.shape[-1]
    normed = low(norm_apply(inputs, gains[0], biases[0]))
    mixed = jnp.dot(normed, w_qkv, precision=highest)
    queries = low_back(low(mixed[:, :feat_width] + biases[1]))
    key_rows = low_back(low(mixed[:, feat_width:2 * feat_width]))
    value_rows = low_back(low(mixed[:, 2 * feat_width:] + biases[2]))
    head_shape = (inputs.shape[0], HEADS, HEAD_DIM)
    scores = jnp.einsum('qhd,khd->hqk', queries.reshape(head_shape), key_rows.reshape(head_shape), precision=highest) * HEAD_DIM ** (-0.5)
    scores = low_back(scores)
    same_clip = clip_row[:, None] == clip_row[None, :]
    scores = jnp.where(same_clip[None], scores, neg_big)
    row_peak = lax.optimization_barrier(jnp.max(scores, axis=-1, keepdims=True))
    exp_scores = jnp.exp(scores - row_peak)
    row_total = lax.optimization_barrier(jnp.sum(exp_scores, axis=-1, keepdims=True))
    probs = low(exp_scores / row_total)
    attended = jnp.einsum('hqk,khd->qhd', probs, value_rows.reshape(head_shape), precision=highest).reshape(inputs.shape)
    attended = low_back(low(attended))
    branch = low_back(jnp.dot(attended, w_out, precision=highest) + biases[3])
    hidden = inputs + branch
    normed_two = low(norm_apply(hidden, gains[1], biases[4]))
    pre_act = low_back(jnp.dot(normed_two, w_up, precision=highest) + up_bias)
    activated = low(gelu_exact(pre_act))
    mlp_out = low_back(jnp.dot(activated, w_down, precision=highest) + biases[5])
    return hidden + mlp_out

def window(inputs, clip_ids, w_qkv, w_out, w_up, w_down, biases, up_bias, gains):
    seq_count = inputs.shape[0] * inputs.shape[1]
    seq_rows = inputs.reshape(seq_count, LEN, D)
    clip_rows = clip_ids.reshape(seq_count, LEN)

    def one_sequence(operands):
        values, clip_row = operands
        middle = encoder_layer(values, clip_row, w_qkv[0], w_out[0], w_up[0], w_down[0], biases[0], up_bias[0], gains[0])
        middle = low_back(low(middle))
        return encoder_layer(middle, clip_row, w_qkv[1], w_out[1], w_up[1], w_down[1], biases[1], up_bias[1], gains[1])
    result = lax.map(jax.checkpoint(one_sequence), (seq_rows, clip_rows))
    return result.reshape(inputs.shape)

def reference(feed, segment_ids, w_qkv, w_out, w_up, w_down, biases, up_bias, gains):
    inputs = feed[0].astype(jnp.float32)
    cotangent = feed[1].astype(jnp.float32)
    params = tuple((param.astype(jnp.float32) for param in (w_qkv, w_out, w_up, w_down, biases, up_bias, gains)))

    def forward(values, wq_full, wo_full, wu_full, wd_full, bias_full, upb_full, gain_full):
        return window(values, segment_ids, wq_full, wo_full, wu_full, wd_full, bias_full, upb_full, gain_full)
    outputs, pullback = jax.vjp(forward, inputs, *params)
    grads = pullback(cotangent)
    section_out = jnp.stack([grads[0], outputs]).astype(jnp.bfloat16)
    return (section_out, grads[1], grads[2], grads[3], grads[4], grads[5], grads[6], grads[7])
```

```python
import jax
import jax.numpy as jnp
from jax import lax
from jax.sharding import PartitionSpec as P

HEAD_DIM = 64


epsilon = 1e-05
neg_big = -1000000000.0


def shifted(block, axis, distance):
    devices = range(lax.axis_size(axis))
    route = [(i - distance, i) for i in devices if i - distance in devices]
    return lax.ppermute(block, axis, route)


def norm_apply(values, gain_row, shift_row):
    row_mean = jnp.mean(values, axis=-1, keepdims=True)
    centred = values - row_mean
    variance = jnp.mean(centred * centred, axis=-1, keepdims=True)
    return centred * lax.rsqrt(variance + epsilon) * gain_row + shift_row


def gelu_exact(values):
    return 0.5 * values * (1.0 + lax.erf(values * 2.0 ** (-0.5)))


def split_heads(head_data):
    batch_rows, length, group_width = (head_data.shape[0], head_data.shape[1], head_data.shape[3])
    split_shape = (batch_rows, length, group_width // HEAD_DIM, HEAD_DIM)
    return (
        head_data[:, :, 0].reshape(split_shape),
        head_data[:, :, 1].reshape(split_shape),
        head_data[:, :, 2].reshape(split_shape),
    )


def block_scores(query_block, key_rows, clip_block, clip_all):
    score_scale = HEAD_DIM ** (-0.5)
    scores = (
        jnp.einsum("bqhd,bkhd->bhqk", query_block, key_rows, preferred_element_type=jnp.float32)
        * score_scale
    )
    same_clip = clip_block[:, None, :, None] == clip_all[:, None, None, :]
    return jnp.where(same_clip, scores, neg_big)


def attend(head_data, clip_all):
    batch_rows, length, group_width = (head_data.shape[0], head_data.shape[1], head_data.shape[3])
    queries, key_rows, value_rows = split_heads(head_data)
    scores = block_scores(queries, key_rows, clip_all, clip_all)
    row_peak = jnp.max(scores, axis=-1, keepdims=True)
    exp_scores = jnp.exp(scores - row_peak)
    row_total = jnp.sum(exp_scores, axis=-1, keepdims=True)
    probs = (exp_scores / row_total).astype(jnp.bfloat16)
    block_out = jnp.einsum("bhqk,bkhd->bqhd", probs, value_rows, preferred_element_type=jnp.float32)
    outputs = block_out.reshape(batch_rows, -1, group_width).astype(jnp.bfloat16)
    totals = (row_peak + jnp.log(row_total))[..., 0]
    return (outputs, totals)


def attend_back(head_data, clip_all, log_total, grad_heads):
    batch_rows, length, group_width = (head_data.shape[0], head_data.shape[1], head_data.shape[3])
    score_scale = HEAD_DIM ** (-0.5)
    queries, key_rows, value_rows = split_heads(head_data)
    grad_attended = grad_heads.reshape(queries.shape)
    block_rows = min(512, length)
    scores = block_scores(queries, key_rows, clip_all, clip_all)
    probs = jnp.exp(scores - log_total[:, :, 0:block_rows, None])
    grad_probs = jnp.einsum(
        "bqhd,bkhd->bhqk", grad_attended, value_rows, preferred_element_type=jnp.float32
    )
    inner_sum = jnp.sum(probs * grad_probs, axis=-1, keepdims=True)
    grad_scores = (probs * (grad_probs - inner_sum)).astype(jnp.bfloat16)
    query_grads = (
        jnp.einsum("bhqk,bkhd->bqhd", grad_scores, key_rows, preferred_element_type=jnp.float32)
        * score_scale
    )
    grad_keys = (
        jnp.einsum("bhqk,bqhd->bkhd", grad_scores, queries, preferred_element_type=jnp.float32)
        * score_scale
    )
    grad_values = jnp.einsum(
        "bhqk,bqhd->bkhd",
        probs.astype(jnp.bfloat16),
        grad_attended,
        preferred_element_type=jnp.float32,
    )
    stacked = jnp.stack([query_grads, grad_keys, grad_values], 2)
    return stacked.reshape(batch_rows, length, 3, group_width).astype(jnp.bfloat16)


def bit_list(sizes):
    bits = []
    for axis, size in sizes:
        for place in reversed(range(size.bit_length() - 1)):
            bits.append((axis, place))
    return bits


def swap_bit(block, axis, place):
    devices = range(lax.axis_size(axis))
    return lax.ppermute(block, axis, [(i, i ^ (1 << place)) for i in devices])


def bit_orders():
    seq_bits = bit_list([("seq", lax.axis_size("seq"))])
    shard_bits = bit_list([("shard", lax.axis_size("shard"))])
    low, high = shard_bits[-1:], shard_bits[:-1]
    return seq_bits + shard_bits, seq_bits + low, low + seq_bits, high[::-1]


def own_bit(axis, place):
    return (lax.axis_index(axis) >> place) & 1


def gather_rows(block, wide_first):
    names, first, second, far = bit_orders()
    wide = first if wide_first else second
    have = []
    data = block
    for axis, place in (wide + far)[::-1]:
        other = swap_bit(data, axis, place)
        mine = own_bit(axis, place) == 0
        order = names.index((axis, place))
        at = sum(1 for h in have if names.index(h) < order)
        data = jnp.stack([jnp.where(mine, data, other), jnp.where(mine, other, data)], at)
        have.append((axis, place))
    return data.reshape((-1,) + block.shape)


def scatter_sum(blocks, wide_first, wire):
    names, first, second, far = bit_orders()
    wide = first if wide_first else second
    have = list(names)
    data = blocks.reshape((2,) * len(names) + blocks.shape[1:])
    for axis, place in wide + far:
        at = have.index((axis, place))
        mine = own_bit(axis, place)
        away = lax.dynamic_index_in_dim(data, 1 - mine, at, keepdims=False).astype(wire)
        kept = lax.dynamic_index_in_dim(data, mine, at, keepdims=False)
        data = kept + swap_bit(away, axis, place).astype(jnp.float32)
        have.remove((axis, place))
    return data


def layer_forward(inputs, clip_all, params):
    w_qkv, w_out, w_up, w_down, biases, up_bias, gains = params
    feat_width = inputs.shape[-1]
    normed = norm_apply(inputs, gains[0], biases[0]).astype(jnp.bfloat16)
    mixed = jnp.einsum("btd,de->bte", normed, w_qkv, preferred_element_type=jnp.float32)
    mixed = mixed.reshape(inputs.shape[0], inputs.shape[1], 3, feat_width)
    mixed = mixed + jnp.stack([biases[1], jnp.zeros_like(biases[1]), biases[2]])
    head_data = lax.all_to_all(
        mixed.astype(jnp.bfloat16), "seq", split_axis=3, concat_axis=1, tiled=True
    )
    attended, log_total = attend(head_data, clip_all)
    tok_out = lax.all_to_all(attended, "seq", split_axis=1, concat_axis=2, tiled=True)
    hidden = (
        inputs
        + jnp.einsum("btd,de->bte", tok_out, w_out, preferred_element_type=jnp.float32)
        + biases[3]
    )
    normed_two = norm_apply(hidden, gains[1], biases[4]).astype(jnp.bfloat16)
    pre_act = (
        jnp.einsum("btd,df->btf", normed_two, w_up, preferred_element_type=jnp.float32) + up_bias
    )
    activated = gelu_exact(pre_act).astype(jnp.bfloat16)
    layer_out = (
        hidden
        + jnp.einsum("btf,fd->btd", activated, w_down, preferred_element_type=jnp.float32)
        + biases[5]
    )
    return (layer_out, (inputs, head_data, log_total, tok_out, hidden, pre_act))


def layer_backward(grad_out, saved_state, clip_all, params):
    inputs, head_data, log_total, tok_out, hidden, pre_act = saved_state
    w_qkv, w_out, w_up, w_down, biases, up_bias, gains = params
    feat_width = inputs.shape[-1]
    grad_mlp = grad_out.astype(jnp.bfloat16)
    activated, gelu_pull = jax.vjp(gelu_exact, pre_act)
    activated = activated.astype(jnp.bfloat16)
    grad_b_down = jnp.sum(grad_mlp.astype(jnp.float32), axis=(0, 1))
    grad_act = jnp.einsum("btd,fd->btf", grad_mlp, w_down, preferred_element_type=jnp.float32)
    grad_pre = gelu_pull(grad_act)[0].astype(jnp.bfloat16)
    grad_up_bias = jnp.sum(grad_pre.astype(jnp.float32), axis=(0, 1))
    normed_two, norm_two_pull = jax.vjp(norm_apply, hidden, gains[1], biases[4])
    normed_two = normed_two.astype(jnp.bfloat16)
    grad_normed_two = jnp.einsum("btf,df->btd", grad_pre, w_up, preferred_element_type=jnp.float32)
    grad_hidden_norm, grad_gain_two, grad_shift_two = norm_two_pull(grad_normed_two)
    grad_hidden = grad_out + grad_hidden_norm
    grad_branch = grad_hidden.astype(jnp.bfloat16)
    grad_b_out = jnp.sum(grad_branch.astype(jnp.float32), axis=(0, 1))
    grad_tok = jnp.einsum(
        "bte,de->btd", grad_branch, w_out, preferred_element_type=jnp.float32
    ).astype(jnp.bfloat16)
    grad_heads = lax.all_to_all(grad_tok, "seq", split_axis=2, concat_axis=1, tiled=True)
    grad_mixed = attend_back(head_data, clip_all, log_total, grad_heads)
    grad_tok_mixed = lax.all_to_all(grad_mixed, "seq", split_axis=1, concat_axis=3, tiled=True)
    grad_b_query = jnp.sum(grad_tok_mixed[:, :, 0].astype(jnp.float32), axis=(0, 1))
    grad_b_value = jnp.sum(grad_tok_mixed[:, :, 2].astype(jnp.float32), axis=(0, 1))
    flat_grad = grad_tok_mixed.reshape(inputs.shape[0], inputs.shape[1], 3 * feat_width)
    normed, norm_one_pull = jax.vjp(norm_apply, inputs, gains[0], biases[0])
    normed = normed.astype(jnp.bfloat16)
    grad_normed = jnp.einsum("bte,de->btd", flat_grad, w_qkv, preferred_element_type=jnp.float32)
    grad_in_norm, grad_gain_one, grad_shift_one = norm_one_pull(grad_normed)
    grad_inputs = grad_hidden + grad_in_norm
    grad_biases = jnp.stack(
        [grad_shift_one, grad_b_query, grad_b_value, grad_b_out, grad_shift_two, grad_b_down]
    )
    grad_gains = jnp.stack([grad_gain_one, grad_gain_two])
    return (
        grad_inputs,
        (activated, grad_mlp, normed_two, grad_pre, tok_out, grad_branch, normed, flat_grad),
        (grad_biases, grad_up_bias, grad_gains),
    )


def rows_product(left, right):
    return jnp.einsum("btd,bte->de", left, right, preferred_element_type=jnp.float32)


def per_device(feed, segment_ids, w_qkv, w_out, w_up, w_down, biases, up_bias, gains):
    section_id = lax.axis_index("section")
    at_first = section_id == 0
    micro_count = feed.shape[1]
    devices = lax.axis_size("seq") * lax.axis_size("shard")
    bias_size, up_size, gain_size = (leaf[0].size for leaf in (biases, up_bias, gains))
    packed = jnp.concatenate([biases[0].ravel(), up_bias[0].ravel(), gains[0].ravel()])
    packed = gather_rows(packed[None], True)[:, 0].astype(jnp.float32)
    width = biases.shape[2]

    def spread(part, count):
        return part.reshape(devices, count, width).swapaxes(0, 1).reshape(count, -1)

    qk_width = 2 * w_qkv.shape[2] // 3
    feat = qk_width // 2
    params = (
        jnp.concatenate(
            [
                gather_rows(w_qkv[0][:, :qk_width], True).reshape(-1, qk_width),
                gather_rows(w_qkv[0][:, qk_width:], False).reshape(-1, feat),
            ],
            1,
        ),
        gather_rows(w_out[0], False).reshape(-1, w_out.shape[2]),
        gather_rows(w_up[0], True).reshape(-1, w_up.shape[2]),
        gather_rows(w_down[0], False).reshape(-1, w_down.shape[2]),
        spread(packed[:, :bias_size], biases.shape[1]),
        packed[:, bias_size : bias_size + up_size].reshape(-1),
        spread(packed[:, bias_size + up_size :], gains.shape[1]),
    )
    clip_ids = lax.all_gather(segment_ids, "seq", axis=2, tiled=True)
    stream = feed[0]
    received = jnp.zeros(stream.shape[1:], jnp.bfloat16)
    saved_list = []
    layer_outs = []
    for clock in range(micro_count + 1):
        own_block = stream[min(clock, micro_count - 1)]
        layer_in = jnp.where(at_first, own_block, received).astype(jnp.float32)
        batch_index = jnp.clip(clock - section_id, 0, micro_count - 1)
        clip_all = lax.dynamic_index_in_dim(clip_ids, batch_index, 0, keepdims=False)
        layer_out, saved_state = layer_forward(layer_in, clip_all, params)
        saved_list.append(saved_state + (clip_all,))
        layer_outs.append(layer_out.astype(jnp.bfloat16))
        if clock < micro_count:
            received = shifted(layer_outs[-1], "section", 1)
    stacked = jax.tree.map(lambda *leaves: jnp.stack(leaves), *saved_list)
    received = jnp.zeros(stream.shape[1:], jnp.bfloat16)
    grad_inputs = []
    pieces_list = []
    totals = None
    for clock in range(micro_count + 1):
        source = jnp.clip(clock - 1 + 2 * section_id, 0, micro_count)
        saved_state = jax.tree.map(
            lambda leaf: lax.dynamic_index_in_dim(leaf, source, 0, keepdims=False), stacked
        )
        is_valid = jnp.where(at_first, clock >= 1, clock < micro_count)
        grad_out = jnp.where(at_first, received, stream[min(clock, micro_count - 1)]).astype(
            jnp.float32
        )
        grad_out = jnp.where(is_valid, grad_out, 0.0)
        grad_in, pieces, grads = layer_backward(
            grad_out, saved_state[:-1], saved_state[-1], params
        )
        pieces_list.append(pieces)
        grad_inputs.append(grad_in.astype(jnp.bfloat16))
        if clock < micro_count:
            received = shifted(grad_inputs[-1], "section", -1)
        totals = grads if totals is None else jax.tree.map(jnp.add, totals, grads)
    (activated, grad_mlp, normed_two, grad_pre, tok_out, grad_branch, normed, flat_grad) = (
        jnp.concatenate(leaves) for leaves in zip(*pieces_list)
    )

    def own_rows(total, wide_first):
        return scatter_sum(
            total.reshape(devices, -1, total.shape[-1]), wide_first, jnp.bfloat16
        )

    grad_w_down = own_rows(rows_product(activated, grad_mlp), True)
    grad_w_up = own_rows(rows_product(normed_two, grad_pre), False)
    grad_w_out = own_rows(rows_product(tok_out, grad_branch), False)
    grad_w_qk = own_rows(rows_product(normed, flat_grad[..., :qk_width]), True)
    grad_w_v = own_rows(rows_product(normed, flat_grad[..., qk_width:]), False)
    grad_w_qkv = jnp.concatenate([grad_w_qk, grad_w_v], -1)

    def unspread(part):
        return part.reshape(-1, devices, width).swapaxes(0, 1).reshape(devices, -1)

    small = jnp.concatenate(
        [unspread(totals[0]), totals[1].reshape(devices, -1), unspread(totals[2])], 1
    )
    small = scatter_sum(small[:, None], True, jnp.float32)[0]
    totals = (
        grad_w_qkv,
        grad_w_out,
        grad_w_up,
        grad_w_down,
        small[:bias_size].reshape(-1, width),
        small[bias_size : bias_size + up_size],
        small[bias_size + up_size :].reshape(-1, width),
    )
    ends = jnp.where(at_first, jnp.stack(grad_inputs[1:]), jnp.stack(layer_outs[1:]))
    return (ends[None],) + tuple((leaf[None] for leaf in totals))


def solution(mesh):
    in_specs = (
        P("section", None, "shard", "seq", None),
        P(None, "shard", "seq"),
        P("section", ("seq", "shard"), None),
        P("section", ("seq", "shard"), None),
        P("section", ("seq", "shard"), None),
        P("section", ("seq", "shard"), None),
        P("section", None, ("seq", "shard")),
        P("section", ("seq", "shard")),
        P("section", None, ("seq", "shard")),
    )
    out_specs = (
        P("section", None, "shard", "seq", None),
        P("section", ("seq", "shard"), None),
        P("section", ("seq", "shard"), None),
        P("section", ("seq", "shard"), None),
        P("section", ("seq", "shard"), None),
        P("section", None, ("seq", "shard")),
        P("section", ("seq", "shard")),
        P("section", None, ("seq", "shard")),
    )
    return jax.shard_map(
        per_device, mesh=mesh, in_specs=in_specs, out_specs=out_specs, check_vma=False
    )
```

```python
import jax
import jax.numpy as jnp
from jax import lax
from jax.experimental import pallas as pl
from jax.experimental.pallas import tpu as pltpu
from jax.sharding import PartitionSpec as P

HEAD_DIM = 64


epsilon = 1e-05
neg_big = -1000000000.0


def shifted(block, axis, distance):
    devices = range(lax.axis_size(axis))
    route = [(i - distance, i) for i in devices if i - distance in devices]
    return lax.ppermute(block, axis, route)


def norm_apply(values, gain_row, shift_row):
    row_mean = jnp.mean(values, axis=-1, keepdims=True)
    centred = values - row_mean
    variance = jnp.mean(centred * centred, axis=-1, keepdims=True)
    return centred * lax.rsqrt(variance + epsilon) * gain_row + shift_row


def gelu_exact(values):
    return 0.5 * values * (1.0 + lax.erf(values * 2.0 ** (-0.5)))


def dot_rows(left, right):
    return lax.dot_general(
        left, right, (((1,), (1,)), ((), ())), preferred_element_type=jnp.float32
    )


def dot_plain(left, right):
    return jnp.dot(left, right, preferred_element_type=jnp.float32)


def attend_kernel(data_ref, column_ref, row_ref, out_ref):
    width = out_ref.shape[-1]
    same_clip = column_ref[...] == row_ref[...]
    for start in range(0, width, HEAD_DIM):
        queries = data_ref[:, start : start + HEAD_DIM]
        key_rows = data_ref[:, width + start : width + start + HEAD_DIM]
        value_rows = data_ref[:, 2 * width + start : 2 * width + start + HEAD_DIM]
        scores = dot_rows(queries, key_rows) * HEAD_DIM ** (-0.5)
        scores = jnp.where(same_clip, scores, neg_big)
        exp_scores = jnp.exp(scores - jnp.max(scores, axis=-1, keepdims=True))
        probs = exp_scores * (1.0 / jnp.sum(exp_scores, axis=-1, keepdims=True))
        block_out = dot_plain(probs.astype(jnp.bfloat16), value_rows)
        out_ref[:, start : start + HEAD_DIM] = block_out.astype(jnp.bfloat16)


def attend_back_kernel(data_ref, grad_ref, column_ref, row_ref, out_ref):
    width = grad_ref.shape[-1]
    score_scale = HEAD_DIM ** (-0.5)
    same_clip = column_ref[...] == row_ref[...]
    for start in range(0, width, HEAD_DIM):
        spans = [slice(at + start, at + start + HEAD_DIM) for at in (0, width, 2 * width)]
        queries, key_rows, value_rows = (data_ref[:, span] for span in spans)
        grad_attended = grad_ref[:, spans[0]]
        scores = jnp.where(same_clip, dot_rows(key_rows, queries) * score_scale, neg_big)
        exp_scores = jnp.exp(scores - jnp.max(scores, axis=0, keepdims=True))
        probs = exp_scores * (1.0 / jnp.sum(exp_scores, axis=0, keepdims=True))
        grad_probs = dot_rows(value_rows, grad_attended)
        inner_sum = jnp.sum(probs * grad_probs, axis=0, keepdims=True)
        grad_scores = probs * (grad_probs - inner_sum)
        grad_queries = dot_plain(grad_scores.T.astype(jnp.bfloat16), key_rows) * score_scale
        grad_keys = dot_plain(grad_scores.astype(jnp.bfloat16), queries) * score_scale
        grad_values = dot_plain(probs.astype(jnp.bfloat16), grad_attended)
        for span, grad in zip(spans, (grad_queries, grad_keys, grad_values)):
            out_ref[:, span] = grad.astype(jnp.bfloat16)


def call_rows(kernel, arrays, clip_all, out_width, products):
    batch_rows, length = clip_all.shape
    arrays = (*arrays, clip_all[:, :, None], clip_all[:, None, :])
    group_width = arrays[0].shape[2] // 3

    def spec(shape):
        return pl.BlockSpec((None,) + tuple(shape[1:]), lambda b: (b, 0, 0))

    out_shape = jax.ShapeDtypeStruct((batch_rows, length, out_width), jnp.bfloat16)
    return pl.pallas_call(
        kernel,
        grid=(batch_rows,),
        out_shape=out_shape,
        in_specs=[spec(array.shape) for array in arrays],
        out_specs=spec(out_shape.shape),
        cost_estimate=pl.CostEstimate(
            flops=2 * products * batch_rows * length * length * group_width,
            bytes_accessed=batch_rows * length * group_width * 16,
            transcendentals=batch_rows * length * length * group_width // HEAD_DIM,
        ),
    )(*arrays)


def to_heads(rows, parts):
    groups = lax.axis_size("seq")
    batch_rows, frames, width = rows.shape
    part = width // parts
    step = part // groups
    blocks = jnp.stack(
        [
            jnp.concatenate(
                [rows[..., p * part + g * step : p * part + (g + 1) * step] for p in range(parts)],
                -1,
            )
            for g in range(groups)
        ]
    )
    blocks = lax.all_to_all(blocks, "seq", split_axis=0, concat_axis=0, tiled=True)
    return jnp.moveaxis(blocks, 0, 1).reshape(batch_rows, groups * frames, -1)


def to_frames(rows, parts):
    groups = lax.axis_size("seq")
    batch_rows, frames, width = rows.shape
    step = width // parts
    blocks = jnp.moveaxis(rows.reshape(batch_rows, groups, frames // groups, width), 1, 0)
    blocks = lax.all_to_all(blocks, "seq", split_axis=0, concat_axis=0, tiled=True)
    return jnp.concatenate(
        [blocks[g][..., p * step : (p + 1) * step] for p in range(parts) for g in range(groups)],
        -1,
    )


def bit_list(sizes):
    bits = []
    for axis, size in sizes:
        for place in reversed(range(size.bit_length() - 1)):
            bits.append((axis, place))
    return bits


def swap_bit(block, axis, place):
    devices = range(lax.axis_size(axis))
    return lax.ppermute(block, axis, [(i, i ^ (1 << place)) for i in devices])


def bit_orders():
    seq_bits = bit_list([("seq", lax.axis_size("seq"))])
    shard_bits = bit_list([("shard", lax.axis_size("shard"))])
    low, high = shard_bits[-1:], shard_bits[:-1]
    return seq_bits + shard_bits, seq_bits + low, low + seq_bits, high[::-1]


def own_bit(axis, place):
    return (lax.axis_index(axis) >> place) & 1


def gather_rows(block, wide_first):
    names, first, second, far = bit_orders()
    wide = first if wide_first else second
    have = []
    data = block
    for axis, place in (wide + far)[::-1]:
        other = swap_bit(data, axis, place)
        mine = own_bit(axis, place) == 0
        order = names.index((axis, place))
        at = sum(1 for h in have if names.index(h) < order)
        data = jnp.stack([jnp.where(mine, data, other), jnp.where(mine, other, data)], at)
        have.append((axis, place))
    return data.reshape((-1,) + block.shape)


def scatter_sum(blocks, wide_first, wire):
    names, first, second, far = bit_orders()
    wide = first if wide_first else second
    have = list(names)
    data = blocks.reshape((2,) * len(names) + blocks.shape[1:])
    for axis, place in wide + far:
        at = have.index((axis, place))
        mine = own_bit(axis, place)
        away = lax.dynamic_index_in_dim(data, 1 - mine, at, keepdims=False).astype(wire)
        kept = lax.dynamic_index_in_dim(data, mine, at, keepdims=False)
        data = kept + swap_bit(away, axis, place).astype(jnp.float32)
        have.remove((axis, place))
    return data


def layer_forward(inputs, clip_all, params):
    w_qkv, w_out, w_up, w_down, biases, up_bias, gains = params
    normed = norm_apply(inputs, gains[0], biases[0]).astype(jnp.bfloat16)
    mixed = jnp.einsum("btd,de->bte", normed, w_qkv, preferred_element_type=jnp.float32)
    mixed = mixed + jnp.concatenate([biases[1], jnp.zeros_like(biases[1]), biases[2]])
    head_data = to_heads(mixed.astype(jnp.bfloat16), 3)
    attended = call_rows(
        attend_kernel, (head_data,), clip_all, head_data.shape[2] // 3, 2
    )
    tok_out = to_frames(attended, 1)
    hidden = (
        inputs
        + jnp.einsum("btd,de->bte", tok_out, w_out, preferred_element_type=jnp.float32)
        + biases[3]
    )
    normed_two = norm_apply(hidden, gains[1], biases[4]).astype(jnp.bfloat16)
    pre_act = (
        jnp.einsum("btd,df->btf", normed_two, w_up, preferred_element_type=jnp.float32) + up_bias
    )
    activated = gelu_exact(pre_act).astype(jnp.bfloat16)
    layer_out = (
        hidden
        + jnp.einsum("btf,fd->btd", activated, w_down, preferred_element_type=jnp.float32)
        + biases[5]
    )
    return (layer_out, (inputs, head_data, tok_out, hidden, pre_act))


def layer_backward(grad_out, saved_state, clip_all, params):
    inputs, head_data, tok_out, hidden, pre_act = saved_state
    w_qkv, w_out, w_up, w_down, biases, up_bias, gains = params
    feat_width = inputs.shape[-1]
    grad_mlp = grad_out.astype(jnp.bfloat16)
    activated, gelu_pull = jax.vjp(gelu_exact, pre_act)
    activated = activated.astype(jnp.bfloat16)
    grad_b_down = jnp.sum(grad_mlp.astype(jnp.float32), axis=(0, 1))
    grad_act = jnp.einsum("btd,fd->btf", grad_mlp, w_down, preferred_element_type=jnp.float32)
    grad_pre = gelu_pull(grad_act)[0].astype(jnp.bfloat16)
    grad_up_bias = jnp.sum(grad_pre.astype(jnp.float32), axis=(0, 1))
    normed_two, norm_two_pull = jax.vjp(norm_apply, hidden, gains[1], biases[4])
    normed_two = normed_two.astype(jnp.bfloat16)
    grad_normed_two = jnp.einsum("btf,df->btd", grad_pre, w_up, preferred_element_type=jnp.float32)
    grad_hidden_norm, grad_gain_two, grad_shift_two = norm_two_pull(grad_normed_two)
    grad_hidden = grad_out + grad_hidden_norm
    grad_branch = grad_hidden.astype(jnp.bfloat16)
    grad_b_out = jnp.sum(grad_branch.astype(jnp.float32), axis=(0, 1))
    grad_tok = jnp.einsum(
        "bte,de->btd", grad_branch, w_out, preferred_element_type=jnp.float32
    ).astype(jnp.bfloat16)
    grad_heads = to_heads(grad_tok, 1)
    grad_mixed = call_rows(
        attend_back_kernel, (head_data, grad_heads), clip_all, head_data.shape[2], 5
    )
    flat_grad = to_frames(grad_mixed, 3)
    grad_b_query = jnp.sum(flat_grad[:, :, :feat_width].astype(jnp.float32), axis=(0, 1))
    grad_b_value = jnp.sum(flat_grad[:, :, 2 * feat_width :].astype(jnp.float32), axis=(0, 1))
    normed, norm_one_pull = jax.vjp(norm_apply, inputs, gains[0], biases[0])
    normed = normed.astype(jnp.bfloat16)
    grad_normed = jnp.einsum("bte,de->btd", flat_grad, w_qkv, preferred_element_type=jnp.float32)
    grad_in_norm, grad_gain_one, grad_shift_one = norm_one_pull(grad_normed)
    grad_inputs = grad_hidden + grad_in_norm
    grad_biases = jnp.stack(
        [grad_shift_one, grad_b_query, grad_b_value, grad_b_out, grad_shift_two, grad_b_down]
    )
    grad_gains = jnp.stack([grad_gain_one, grad_gain_two])
    return (
        grad_inputs,
        (activated, grad_mlp, normed_two, grad_pre, tok_out, grad_branch, normed, flat_grad),
        (grad_biases, grad_up_bias, grad_gains),
    )


def rows_product(left, right):
    return jnp.einsum("btd,bte->de", left, right, preferred_element_type=jnp.float32)


def per_device(feed, segment_ids, w_qkv, w_out, w_up, w_down, biases, up_bias, gains):
    section_id = lax.axis_index("section")
    at_first = section_id == 0
    micro_count = feed.shape[1]
    devices = lax.axis_size("seq") * lax.axis_size("shard")
    bias_size, up_size, gain_size = (leaf[0].size for leaf in (biases, up_bias, gains))
    packed = jnp.concatenate([biases[0].ravel(), up_bias[0].ravel(), gains[0].ravel()])
    packed = gather_rows(packed[None], True)[:, 0].astype(jnp.float32)
    width = biases.shape[2]

    def spread(part, count):
        return part.reshape(devices, count, width).swapaxes(0, 1).reshape(count, -1)

    qk_width = 2 * w_qkv.shape[2] // 3
    feat = qk_width // 2
    params = (
        jnp.concatenate(
            [
                gather_rows(w_qkv[0][:, :qk_width], True).reshape(-1, qk_width),
                gather_rows(w_qkv[0][:, qk_width:], False).reshape(-1, feat),
            ],
            1,
        ),
        gather_rows(w_out[0], False).reshape(-1, w_out.shape[2]),
        gather_rows(w_up[0], True).reshape(-1, w_up.shape[2]),
        gather_rows(w_down[0], False).reshape(-1, w_down.shape[2]),
        spread(packed[:, :bias_size], biases.shape[1]),
        packed[:, bias_size : bias_size + up_size].reshape(-1),
        spread(packed[:, bias_size + up_size :], gains.shape[1]),
    )
    clip_ids = lax.all_gather(segment_ids, "seq", axis=2, tiled=True)
    stream = feed[0]
    received = jnp.zeros(stream.shape[1:], jnp.bfloat16)
    saved_list = []
    layer_outs = []
    for clock in range(micro_count + 1):
        own_block = stream[min(clock, micro_count - 1)]
        layer_in = jnp.where(at_first, own_block, received).astype(jnp.float32)
        batch_index = jnp.clip(clock - section_id, 0, micro_count - 1)
        clip_all = lax.dynamic_index_in_dim(clip_ids, batch_index, 0, keepdims=False)
        layer_out, saved_state = layer_forward(layer_in, clip_all, params)
        saved_list.append(saved_state + (clip_all,))
        layer_outs.append(layer_out.astype(jnp.bfloat16))
        if clock < micro_count:
            received = shifted(layer_outs[-1], "section", 1)
    stacked = jax.tree.map(lambda *leaves: jnp.stack(leaves), *saved_list)
    received = jnp.zeros(stream.shape[1:], jnp.bfloat16)
    grad_inputs = []
    pieces_list = []
    totals = None
    for clock in range(micro_count + 1):
        source = jnp.clip(clock - 1 + 2 * section_id, 0, micro_count)
        saved_state = jax.tree.map(
            lambda leaf: lax.dynamic_index_in_dim(leaf, source, 0, keepdims=False), stacked
        )
        is_valid = jnp.where(at_first, clock >= 1, clock < micro_count)
        grad_out = jnp.where(at_first, received, stream[min(clock, micro_count - 1)]).astype(
            jnp.float32
        )
        grad_out = jnp.where(is_valid, grad_out, 0.0)
        grad_in, pieces, grads = layer_backward(
            grad_out, saved_state[:-1], saved_state[-1], params
        )
        pieces_list.append(pieces)
        grad_inputs.append(grad_in.astype(jnp.bfloat16))
        if clock < micro_count:
            received = shifted(grad_inputs[-1], "section", -1)
        totals = grads if totals is None else jax.tree.map(jnp.add, totals, grads)
    (activated, grad_mlp, normed_two, grad_pre, tok_out, grad_branch, normed, flat_grad) = (
        jnp.concatenate(leaves) for leaves in zip(*pieces_list)
    )

    def own_rows(total, wide_first):
        return scatter_sum(
            total.reshape(devices, -1, total.shape[-1]), wide_first, jnp.bfloat16
        )

    grad_w_down = own_rows(rows_product(activated, grad_mlp), True)
    grad_w_up = own_rows(rows_product(normed_two, grad_pre), False)
    grad_w_out = own_rows(rows_product(tok_out, grad_branch), False)
    grad_w_qk = own_rows(rows_product(normed, flat_grad[..., :qk_width]), True)
    grad_w_v = own_rows(rows_product(normed, flat_grad[..., qk_width:]), False)
    grad_w_qkv = jnp.concatenate([grad_w_qk, grad_w_v], -1)

    def unspread(part):
        return part.reshape(-1, devices, width).swapaxes(0, 1).reshape(devices, -1)

    small = jnp.concatenate(
        [unspread(totals[0]), totals[1].reshape(devices, -1), unspread(totals[2])], 1
    )
    small = scatter_sum(small[:, None], True, jnp.float32)[0]
    totals = (
        grad_w_qkv,
        grad_w_out,
        grad_w_up,
        grad_w_down,
        small[:bias_size].reshape(-1, width),
        small[bias_size : bias_size + up_size],
        small[bias_size + up_size :].reshape(-1, width),
    )
    ends = jnp.where(at_first, jnp.stack(grad_inputs[1:]), jnp.stack(layer_outs[1:]))
    return (ends[None],) + tuple((leaf[None] for leaf in totals))


def solution(mesh):
    in_specs = (
        P("section", None, "shard", "seq", None),
        P(None, "shard", "seq"),
        P("section", ("seq", "shard"), None),
        P("section", ("seq", "shard"), None),
        P("section", ("seq", "shard"), None),
        P("section", ("seq", "shard"), None),
        P("section", None, ("seq", "shard")),
        P("section", ("seq", "shard")),
        P("section", None, ("seq", "shard")),
    )
    out_specs = (
        P("section", None, "shard", "seq", None),
        P("section", ("seq", "shard"), None),
        P("section", ("seq", "shard"), None),
        P("section", ("seq", "shard"), None),
        P("section", ("seq", "shard"), None),
        P("section", None, ("seq", "shard")),
        P("section", ("seq", "shard")),
        P("section", None, ("seq", "shard")),
    )
    return jax.shard_map(
        per_device, mesh=mesh, in_specs=in_specs, out_specs=out_specs, check_vma=False
    )
```
